512 devices in a mesh: db: 64 (over z, x), seq: 8 (over y, core).
Axes of the slice: x: 4, y: 4, z: 16, core: 2. Of those that a mesh axis runs over, the one named last changes fastest.
Arguments:
- reader: bfloat16 [64, 1024, 2048], P('db', 'seq'), may hold values from -6 to 6
- reader_gain: float32 [2048], replicated, may hold values from 0.1 to 1.9
- database: bfloat16 [8192, 2, 896], P('db')
- encoder_gain: float32 [896], replicated, may hold values from 0.1 to 1.9
- w_expand: bfloat16 [896, 1792], P('db', 'seq'), may hold values from -0.1875 to 0.1875
- w_reduce: bfloat16 [1792, 896], P('seq', 'db'), may hold values from -0.125 to 0.125
- w_query: bfloat16 [2048, 2048], P('db', 'seq'), may hold values from -0.125 to 0.125
- w_key: bfloat16 [896, 2048], P('db', 'seq'), may hold values from -0.1875 to 0.1875
- w_value: bfloat16 [896, 2048], P('db', 'seq'), may hold values from -0.1875 to 0.1875
- w_output: bfloat16 [2048, 2048], P('db', 'seq'), may hold values from -0.125 to 0.125
- neighbour_ids: int32 [64, 8, 4], replicated, may hold values from 0 to 127
- lengths: int32 [64, 8, 4], P('db'), may hold values from 1 to 128, 320 in all within a row
- owners: int32 [64, 8, 4], P('db'), may hold values from 0 to 63
Outputs:
- updated: bfloat16 [64, 1024, 2048], P('db', None, 'seq')
The draws below stay inside these ranges and needn't reach their ends.
Inputs may be any that keep to these rules, and one draw needn't show every extreme that they name: For every sequence b and every q, the lengths[b, q, :] of its 4 neighbours sum to exactly 320, and the longest of them is 128.
All inputs are finite; a program needn't handle non-finite values.
Results may differ from the reference program's by a relative error of at most 0.0065.
The reference program's roundings to bfloat16 on the way count: a program that leaves them out, or rounds other values in their place, can miss the bound.
Values may be sent and summed in bfloat16 or wider, within the bound.
No kernel may reach another device: no remote copies, remote signals or barrier semaphores. Data moves between devices by JAX's collectives and lax.ppermute only.
A program may use at most 64 MiB of HBM per device.

```python
import math
import jax
import jax.numpy as jnp
import numpy as np
from jax import lax

D = 2048
HEADS = 16
HD = 128
HW = 2048
DE = 896
FFH = 1792
SPAN = 64
KNN = 2
RL = 128
CH_DEV = 2
NBR_DEV = 4
PACK = 320
STRIPE = 2
ENTRIES = 128
SEQ = 1024
N_DB = 64
N_SEQ = 8


def draw_database(key, part):
    first, second = jax.random.split(key, 2)
    shape = (N_DB * ENTRIES, STRIPE, DE)
    base = jax.random.normal(first, shape, jnp.float32)
    spread = jnp.exp(jax.random.uniform(second, (N_DB * ENTRIES, STRIPE, 1), jnp.float32, -0.7, 0.7))
    values = base * spread
    return jnp.clip(values, -300.0, 300.0).astype(jnp.bfloat16)


def with_ends(values, key, low, top_value):
    place = [jax.random.randint(jax.random.fold_in(key, axis), (), 0, length) for axis, length in enumerate(values.shape)]
    widest = values.shape.index(max(values.shape))
    beside = place[:widest] + [(place[widest] + 1) % values.shape[widest]] + place[widest + 1:]
    return values.at[tuple(place)].set(low).at[tuple(beside)].set(top_value)


def shard_levels(rng, dims, shards, low, high):
    def one(position, parts):
        heights = jax.random.uniform(jax.random.fold_in(jax.random.fold_in(rng, 6), position), (parts,), jnp.float32, low / len(shards), high / len(shards))
        return jnp.repeat(jnp.exp(heights), dims[position] // parts).reshape((-1,) + (1,) * (len(dims) - position - 1))

    factor_of = one(*shards[0])
    for cut in shards[1:]:
        factor_of = factor_of * one(*cut)
    return factor_of


def profile(count, total, most, lean):
    weights = [(1 << 20) // math.isqrt(rank ** lean) + 1 for rank in range(2, count + 1)]
    spare, given = total - most - (count - 1), [1] * (count - 1)
    while spare > 0:
        movable = [i for i in range(count - 1) if given[i] < most]
        mass, left = sum([weights[i] for i in movable]), spare
        for i in movable:
            extra = min(most - given[i], max(1, left * weights[i] // mass), spare)
            given[i] = given[i] + extra
            spare = spare - extra
    return np.array([most] + given)


def uneven(rng, amount, total, limit, lean):
    if amount == 2:
        one = jax.random.randint(rng, (), max(1, total - limit), min(limit, total - 1) + 1)
        return jnp.stack([one, total - one])
    sizes = jnp.asarray(profile(amount, total, limit, lean), jnp.int32)
    twos = (amount - 1) // 2
    donor, taker = sizes[1:1 + 2 * twos:2], sizes[2:2 + 2 * twos:2]
    room = jnp.minimum(donor - 1, limit - taker)
    shifted = jax.random.randint(jax.random.fold_in(rng, 1), (twos,), 0, 1 << 20) % (room + 1)
    sizes = sizes.at[1:1 + 2 * twos:2].set(donor - shifted).at[2:2 + 2 * twos:2].set(taker + shifted)
    return sizes[jax.random.permutation(jax.random.fold_in(rng, 2), amount)]


def gaussian(stream_key, dims, deviation, reach, cuts=(), kind=jnp.bfloat16):
    drawn = deviation * jax.random.normal(stream_key, dims, jnp.float32)
    if cuts:
        drawn = drawn * shard_levels(stream_key, dims, cuts, -0.22, 0.18)
    return jnp.clip(drawn, -reach, reach).astype(kind)


def setup_inputs(seed: int = 0) -> dict:
    keys = jax.random.split(jax.random.key(seed), 14)
    reader = gaussian(keys[0], (N_DB, SEQ, D), 1.0, 6.0, ((0, 64), (1, 8)))
    reader_gain = jnp.clip(1.0 + 0.18 * jax.random.normal(keys[1], (D,), jnp.float32), 0.1, 1.9)
    database = draw_database(jax.random.fold_in(keys[13], 71), 0)
    encoder_gain = jnp.clip(1.0 + 0.18 * jax.random.normal(keys[3], (DE,), jnp.float32), 0.1, 1.9)
    w_expand = gaussian(keys[4], (DE, FFH), DE ** -0.5, 0.1875, ((0, 64), (1, 8)))
    w_reduce = gaussian(keys[5], (FFH, DE), FFH ** -0.5, 0.125, ((0, 8), (1, 64)))
    w_query = gaussian(keys[6], (D, HW), D ** -0.5, 0.125, ((0, 64), (1, 8)))
    w_key = gaussian(keys[7], (DE, HW), DE ** -0.5, 0.1875, ((0, 64), (1, 8)))
    w_value = gaussian(keys[8], (DE, HW), DE ** -0.5, 0.1875, ((0, 64), (1, 8)))
    w_output = gaussian(keys[9], (HW, D), HW ** -0.5, 0.125, ((0, 64), (1, 8)))
    neighbour_ids = with_ends(jax.random.randint(keys[10], (N_DB, N_SEQ, NBR_DEV), 0, ENTRIES), jax.random.fold_in(keys[10], 1), 0, ENTRIES - 1).astype(jnp.int32)
    lengths = jax.vmap(lambda own: uneven(own, NBR_DEV, PACK, RL, 2))(jax.random.split(keys[11], N_DB * N_SEQ)).reshape((N_DB, N_SEQ, NBR_DEV)).astype(jnp.int32)
    owners = with_ends(jax.random.randint(keys[12], (N_DB, N_SEQ, NBR_DEV), 0, N_DB), jax.random.fold_in(keys[12], 1), 0, N_DB - 1).astype(jnp.int32)
    return dict(reader=reader, reader_gain=reader_gain, database=database, encoder_gain=encoder_gain, w_expand=w_expand, w_reduce=w_reduce, w_query=w_query, w_key=w_key, w_value=w_value, w_output=w_output, neighbour_ids=neighbour_ids, lengths=lengths, owners=owners)


epsilon = 1e-06

def rms_scale(values, scales):
    widened = values.astype(jnp.float32)
    mean_square = lax.optimization_barrier(jnp.mean(widened * widened, axis=-1, keepdims=True))
    return widened * lax.rsqrt(mean_square + epsilon) * scales

def encode_rows(stored, encoder_gain, w_expand, w_reduce, w_pairs):
    normed = rms_scale(stored, encoder_gain).astype(jnp.bfloat16)
    hidden = jax.nn.gelu(jnp.dot(normed, w_expand, preferred_element_type=jnp.float32), approximate=False).astype(jnp.bfloat16)
    encoded = (stored.astype(jnp.float32) + jnp.dot(hidden, w_reduce, preferred_element_type=jnp.float32)).astype(jnp.bfloat16)
    return jnp.dot(encoded, w_pairs, preferred_element_type=jnp.float32).astype(jnp.bfloat16)

def attend(queries, key_value, allowed):
    count = queries.shape[0]
    keys_total = key_value.shape[0]
    query_heads = queries.reshape(count, HEADS, HD).astype(jnp.float32)
    key_heads = key_value[:, :HW].reshape(keys_total, HEADS, HD).astype(jnp.float32)
    value_heads = key_value[:, HW:].reshape(keys_total, HEADS, HD).astype(jnp.float32)
    scores = jnp.einsum('qhd,khd->hqk', query_heads, key_heads) * HD ** (-0.5)
    masked = jnp.where(allowed[None], scores, -jnp.inf)
    largest = lax.optimization_barrier(jnp.max(masked, axis=-1, keepdims=True))
    largest = jnp.where(jnp.isfinite(largest), largest, 0.0)
    powers = jnp.exp(masked - largest)
    totals = lax.optimization_barrier(jnp.sum(powers, axis=-1, keepdims=True))
    weights = (powers / jnp.where(totals > 0, totals, 1.0)).astype(jnp.bfloat16)
    attended = jnp.einsum('hqk,khd->qhd', weights.astype(jnp.float32), value_heads)
    return attended.reshape(count, HW).astype(jnp.bfloat16)

def reference(reader, reader_gain, database, encoder_gain, w_expand, w_reduce, w_query, w_key, w_value, w_output, neighbour_ids, lengths, owners):
    w_pairs = jnp.concatenate([w_key, w_value], axis=1)
    stored = database.reshape(N_DB, ENTRIES * STRIPE, DE)

    def encode_block(block):
        return encode_rows(block, encoder_gain, w_expand, w_reduce, w_pairs)
    table_pairs = lax.map(encode_block, stored).reshape(N_DB * ENTRIES, STRIPE, 2 * HW)
    positions = jnp.arange(RL, dtype=jnp.int32)
    window = KNN * RL
    spans_total = N_SEQ * CH_DEV

    def one_sequence(item):
        tokens, ids_rows, length_rows, owner_rows = item
        ids_flat = ids_rows.reshape(-1).astype(jnp.int32)
        length_flat = length_rows.reshape(-1).astype(jnp.int32)
        owner_flat = owner_rows.reshape(-1).astype(jnp.int32)
        shard = (owner_flat[:, None] + positions[None, :] // STRIPE) % N_DB
        row_select = shard * ENTRIES + ids_flat[:, None]
        gathered = table_pairs[row_select, (positions % STRIPE)[None, :]]
        live = positions[None, :] < length_flat[:, None]
        span_pairs = gathered.reshape(spans_total, window, 2 * HW)
        span_live = live.reshape(spans_total, window)
        prior_pairs = jnp.concatenate([jnp.zeros((1, window, 2 * HW), jnp.bfloat16), span_pairs[:-1]], axis=0)
        prior_live = jnp.concatenate([jnp.zeros((1, window), bool), span_live[:-1]], axis=0)
        normed = rms_scale(tokens, reader_gain).astype(jnp.bfloat16)
        queries = jnp.dot(normed, w_query, preferred_element_type=jnp.float32).astype(jnp.bfloat16)
        query_spans = queries.reshape(spans_total, SPAN, HW)
        allowed = jnp.broadcast_to(prior_live[:, None, :], (spans_total, SPAN, window))
        attended = jax.vmap(attend)(query_spans, prior_pairs, allowed).reshape(SEQ, HW)
        update = jnp.dot(attended, w_output, preferred_element_type=jnp.float32)
        return (tokens.astype(jnp.float32) + update).astype(jnp.bfloat16)
    return lax.map(one_sequence, (reader, neighbour_ids, lengths, owners))
```

```python
import jax
import jax.numpy as jnp
from jax import lax
from jax.sharding import Mesh, PartitionSpec as P

HD = 128
SPAN = 64
KNN = 2
NZ = 16
NX = 4
NY = 4
NC = 2
PACK = 320
DB = ("z", "x")
SEQ = ("y", "c")


epsilon = 1e-06


def rms_scale(values, scales):
    widened = values.astype(jnp.float32)
    mean_square = jnp.mean(widened * widened, axis=-1, keepdims=True)
    return widened * lax.rsqrt(mean_square + epsilon) * scales


def dot(a, b):
    return jnp.dot(a, b, preferred_element_type=jnp.float32)


def spread(part, axis, size):
    copies = jnp.broadcast_to(part[None], (size,) + part.shape)
    return lax.all_to_all(copies, axis, split_axis=0, concat_axis=0, tiled=True)


def ring(step):
    return [(i, (i + step) % NY) for i in range(NY)]


def gather_seq(part):
    half = part.shape[0] // 2
    left = lax.ppermute(part, "y", ring(-1))
    right = lax.ppermute(part, "y", ring(1))
    far_left = lax.ppermute(left[half:], "y", ring(-1))
    far_right = lax.ppermute(right[:half], "y", ring(1))
    far = jnp.concatenate([far_right, far_left], axis=0)
    mine = jnp.stack([part, left, far, right])
    other = lax.ppermute(mine, "c", [(0, 1), (1, 0)])
    return mine, other


def to_natural(mine, other):
    y = lax.axis_index("y")
    c = lax.axis_index("c")
    both = jnp.stack([mine, other], axis=1)
    both = jnp.where(c == 1, both[:, ::-1], both)
    both = jnp.where(y % 2 == 1, jnp.roll(both, 1, axis=0), both)
    both = jnp.where(y // 2 == 1, jnp.roll(both, 2, axis=0), both)
    return both.reshape((NY * NC,) + mine.shape[1:])


def to_relative(blocks):
    y = lax.axis_index("y")
    c = lax.axis_index("c")
    both = blocks.reshape((NY, NC) + blocks.shape[1:])
    both = jnp.where(c == 1, both[:, ::-1], both)
    both = jnp.where(y % 2 == 1, jnp.roll(both, -1, axis=0), both)
    both = jnp.where(y // 2 == 1, jnp.roll(both, -2, axis=0), both)
    return jnp.swapaxes(both, 0, 1).reshape(blocks.shape)


def pad_rows(a, rows):
    return jnp.pad(a, ((0, rows - a.shape[0]), (0, 0)))


def body(
    reader,
    reader_gain,
    database,
    encoder_gain,
    w_expand,
    w_reduce,
    w_query,
    w_key,
    w_value,
    w_output,
    neighbour_ids,
    lengths,
    owners,
):
    bf16 = jnp.bfloat16
    shards = NZ * NX
    seq_index = lax.axis_index("y") * NC + lax.axis_index("c")
    entries, stripe, features = database.shape
    per_row = neighbour_ids.shape[2]

    ids = lax.dynamic_index_in_dim(neighbour_ids, seq_index, 1, keepdims=False)
    token_row = (ids[:, :, None] * stripe + jnp.arange(stripe, dtype=jnp.int32)).reshape(-1)
    stored = database.reshape(entries * stripe, features)
    pick = (token_row[:, None] == jnp.arange(entries * stripe, dtype=jnp.int32)[None]).astype(bf16)
    outgoing = dot(pick, stored).astype(bf16).reshape(shards, per_row * stripe, features)
    arrived = lax.all_to_all(outgoing, DB, split_axis=0, concat_axis=0, tiled=True)
    arrived = arrived.reshape(shards * per_row * stripe, features)

    rows_each = w_expand.shape[0]
    padded = 16
    ff_part = pad_rows(jnp.concatenate([w_expand, w_reduce.T], axis=1), padded)
    ff_cols = spread(spread(ff_part, "z", NZ), "x", NX).reshape(shards * padded, -1)
    slot = jnp.arange(shards * padded, dtype=jnp.int32)
    slot_shard = (slot // padded) % NZ * NX + slot // (padded * NZ)
    slot_feature = jnp.where(slot % padded < rows_each, slot_shard * rows_each + slot % padded, -1)
    place = (slot_feature[:, None] == jnp.arange(features, dtype=jnp.int32)[None]).astype(bf16)
    ff_t = lax.dot_general(
        ff_cols, place, (((0,), (0,)), ((), ())), preferred_element_type=jnp.float32
    ).astype(bf16)
    ff_mine, ff_other = gather_seq(ff_t)
    ff_all = jnp.concatenate([ff_mine, ff_other], axis=0)
    hidden_each = w_expand.shape[1]
    expand_t = ff_all[:, :hidden_each].reshape(-1, features)
    reduce_all = ff_all[:, hidden_each:].reshape(-1, features)

    head_part = jnp.concatenate(
        [
            jnp.concatenate([w_query, w_output], axis=1),
            pad_rows(jnp.concatenate([w_key, w_value], axis=1), padded),
        ],
        axis=0,
    )
    heads = spread(spread(head_part, "z", NZ), "x", NX).reshape((NX, NZ) + head_part.shape)
    model_each = w_query.shape[0]
    width = w_query.shape[1]
    q_o = jnp.swapaxes(heads[:, :, :model_each], 0, 1).reshape(-1, 2 * width)
    w_q = q_o[:, :width]
    w_o = to_relative(q_o[:, width:].reshape(NY * NC, -1, width)).reshape(-1, width)
    pairs = heads[:, :, model_each:].reshape(shards * padded, 2 * width)
    w_pairs = lax.dot_general(
        place, pairs, (((0,), (0,)), ((), ())), preferred_element_type=jnp.float32
    ).astype(bf16)

    own_rows, other_rows = gather_seq(reader[0])
    rows = jnp.concatenate([own_rows, other_rows], axis=0)
    tokens = rows.shape[1]
    normed = rms_scale(rows, reader_gain).astype(bf16).reshape(-1, rows.shape[2])
    queries = dot(normed, w_q).astype(bf16).reshape(2, NY, tokens, width)
    queries = to_natural(queries[0], queries[1]).reshape(-1, width)
    queries = jnp.concatenate([queries[SPAN:], queries[:SPAN]], axis=0)
    queries = to_relative(queries.reshape(NY * NC, tokens, width))
    residual = lax.dynamic_slice_in_dim(rows, seq_index * width, width, 2)
    residual = to_natural(residual[:NY], residual[NY:]).reshape(-1, width)

    own_len = lax.dynamic_index_in_dim(lengths[0], seq_index, 0, keepdims=False)
    own_owner = lax.dynamic_index_in_dim(owners[0], seq_index, 0, keepdims=False)
    position = jnp.arange(PACK, dtype=jnp.int32)
    start = jnp.int32(0)
    source_row = jnp.zeros((PACK,), jnp.int32)
    for j in range(per_row):
        token = position - start
        inside = (token >= 0) & (token < own_len[j])
        shard = (own_owner[j] + token // stripe) % shards
        source = (shard * per_row + j) * stripe + token % stripe
        source_row = jnp.where(inside, source, source_row)
        start = start + own_len[j]
    slots = jnp.arange(arrived.shape[0], dtype=jnp.int32)
    packing = (source_row[:, None] == slots[None]).astype(bf16)
    live_rows = dot(packing, arrived).astype(bf16)

    normed_rows = rms_scale(live_rows, encoder_gain).astype(bf16)
    hidden = lax.dot_general(
        normed_rows, expand_t, (((1,), (1,)), ((), ())), preferred_element_type=jnp.float32
    )
    hidden = jax.nn.gelu(hidden, approximate=False).astype(bf16)
    encoded = (live_rows.astype(jnp.float32) + dot(hidden, reduce_all)).astype(bf16)

    enc_mine, enc_other = gather_seq(encoded)
    enc_all = jnp.concatenate([enc_mine, enc_other], axis=0).reshape(-1, features)
    key_value = dot(enc_all, w_pairs).astype(bf16).reshape(NY * NC, PACK, 2 * width)

    local_heads = width // HD
    keys = key_value[:, :, :width].reshape(NY * NC, PACK, local_heads, HD)
    values = key_value[:, :, width:].reshape(NY * NC, PACK, local_heads, HD)
    first_live = to_relative(lengths[0, :, 0] + lengths[0, :, 1])
    in_first = position[None, :] < first_live[:, None]
    upper = jnp.arange(tokens, dtype=jnp.int32) < SPAN
    allowed = in_first[:, None, :] == upper[None, :, None]
    query_heads = queries.reshape(NY * NC, tokens, local_heads, HD)
    scores = jnp.einsum(
        "cqhd,ckhd->chqk", query_heads, keys, preferred_element_type=jnp.float32
    ) * HD ** (-0.5)
    masked = jnp.where(allowed[:, None], scores, -jnp.inf)
    largest = jnp.max(masked, axis=-1, keepdims=True)
    largest = jnp.where(jnp.isfinite(largest), largest, 0.0)
    powers = jnp.exp(masked - largest)
    totals = jnp.sum(powers, axis=-1, keepdims=True)
    weights = (powers / jnp.where(totals > 0, totals, 1.0)).astype(bf16)
    attended = jnp.einsum("chqk,ckhd->cqhd", weights, values, preferred_element_type=jnp.float32)
    attended = attended.astype(bf16).reshape(NC, NY, tokens, width)
    attended = to_natural(attended[0], attended[1]).reshape(-1, width)
    attended = jnp.concatenate(
        [jnp.zeros((SPAN, width), bf16), attended[: attended.shape[0] - SPAN]], axis=0
    )

    att_mine, att_other = gather_seq(attended)
    att = jnp.concatenate([att_mine, att_other], axis=0)
    att = jnp.swapaxes(att, 0, 1).reshape(att.shape[1], -1)
    update = dot(att, w_o)
    return (residual.astype(jnp.float32) + update).astype(bf16)[None]


def solution(mesh):
    fine = Mesh(mesh.devices.reshape(NZ, NX, NY, NC), ("z", "x", "y", "c"))
    in_specs = (
        P(DB, SEQ, None),
        P(),
        P(DB, None, None),
        P(),
        P(DB, SEQ),
        P(SEQ, DB),
        P(DB, SEQ),
        P(DB, SEQ),
        P(DB, SEQ),
        P(DB, SEQ),
        P(),
        P(DB, None, None),
        P(DB, None, None),
    )
    out_specs = P(DB, None, SEQ)
    return jax.shard_map(body, mesh=fine, in_specs=in_specs, out_specs=out_specs, check_vma=False)
```

```python
import jax
import jax.numpy as jnp
from jax import lax
from jax.experimental import pallas as pl
from jax.experimental.pallas import tpu as pltpu
from jax.sharding import Mesh, PartitionSpec as P

HD = 128
SPAN = 64
NZ = 16
NX = 4
NY = 4
NC = 2
PACK = 320
DB = ("z", "x")
SEQ = ("y", "c")


epsilon = 1e-06


def rms_scale(values, scales):
    widened = values.astype(jnp.float32)
    mean_square = jnp.mean(widened * widened, axis=-1, keepdims=True)
    return widened * lax.rsqrt(mean_square + epsilon) * scales


def dot(a, b):
    return jnp.dot(a, b, preferred_element_type=jnp.float32)


def exchange(blocks, axis):
    return lax.all_to_all(blocks, axis, split_axis=0, concat_axis=0, tiled=True)


def spread(part, axis, size):
    return exchange(jnp.broadcast_to(part[None], (size,) + part.shape), axis)


def ring(step):
    return [(i, (i + step) % NY) for i in range(NY)]


def gather_seq(part):
    swap = [(0, 1), (1, 0)]
    near = lax.ppermute(part, "y", ring(-1))
    last = lax.ppermute(part, "y", ring(1))
    far = lax.ppermute(part, "y", ring(2))
    mine = [part, near, far, last]
    return mine + [lax.ppermute(piece, "c", swap) for piece in mine]


def gather_x(part):
    hops = (-1, 2, 1)
    return [part] + [
        lax.ppermute(part, "x", [(i, (i + step) % NX) for i in range(NX)])
        for step in hops
    ]


def natural_columns():
    return ((lax.axis_index("x") + jnp.arange(NX, dtype=jnp.int32)) % NX).astype(jnp.int32)


def natural_places():
    y = lax.axis_index("y")
    c = lax.axis_index("c")
    ahead = (y + jnp.arange(NY, dtype=jnp.int32)) % NY * NC
    return jnp.concatenate([ahead + c, ahead + 1 - c]).astype(jnp.int32)


def call(kernel, out_shape, operands, scalars, flops, scratch=()):
    size = sum(o.size * o.dtype.itemsize for o in operands)
    return pl.pallas_call(
        kernel,
        out_shape=out_shape,
        in_specs=[pl.BlockSpec(memory_space=pltpu.SMEM)] * scalars
        + [pl.BlockSpec(memory_space=pltpu.VMEM)] * (len(operands) - scalars),
        scratch_shapes=list(scratch),
        cost_estimate=pl.CostEstimate(flops=flops, bytes_accessed=size, transcendentals=0),
    )(*operands)


NT = (((1,), (1,)), ((), ()))


def feed_forward_kernel(rows_ref, gain_ref, *refs):
    pieces, out_ref = refs[:-1], refs[-1]
    each = pieces[0].shape[0] // 2
    rows = rows_ref[...]
    normed = rms_scale(rows, gain_ref[...]).astype(jnp.bfloat16)
    total = rows.astype(jnp.float32)
    for piece in pieces:
        hidden = lax.dot_general(normed, piece[:each], NT, preferred_element_type=jnp.float32)
        hidden = 0.5 * hidden * (1.0 + lax.erf(hidden * 0.5**0.5))
        total = total + dot(hidden.astype(jnp.bfloat16), piece[each:])
    out_ref[...] = total.astype(jnp.bfloat16)


def feature_slots(column, rows_each, slots, axis):
    shape = (1, slots) if axis == 1 else (slots, 1)
    slot = lax.broadcasted_iota(jnp.int32, shape, axis)
    shard = (slot >> 4) * NX + column
    return jnp.where((slot & 15) < rows_each, shard * rows_each + (slot & 15), -1)


def arrange_kernel(column_ref, *refs):
    pieces, out_ref = refs[:-1], refs[-1]
    features = out_ref.shape[1]
    slots = NZ * 16
    total = jnp.zeros(out_ref.shape, jnp.float32)
    for j, piece in enumerate(pieces):
        held = feature_slots(column_ref[j], features // (NZ * NX), slots, 0)
        place = lax.broadcasted_iota(jnp.int32, (slots, features), 1) == held
        total = total + lax.dot_general(
            piece[...].reshape(slots, -1),
            place.astype(jnp.bfloat16),
            (((0,), (0,)), ((), ())),
            preferred_element_type=jnp.float32,
        )
    out_ref[...] = total.astype(jnp.bfloat16)


def query_kernel(place_ref, column_ref, gain_ref, *refs):
    head_pieces, pieces = refs[:NX], refs[NX : NX + NY * NC]
    query_ref, residual_ref, pairs_ref, w_ref = refs[NX + NY * NC :]
    width = w_ref.shape[1]
    features = pairs_ref.shape[0]
    slots = NZ * 16
    total = jnp.zeros(pairs_ref.shape, jnp.float32)
    for j, piece in enumerate(head_pieces):
        column = column_ref[j]
        for z in range(NZ):
            at = pl.multiple_of((z * NX + column) * 32, 32)
            w_ref[pl.ds(at, 16)] = piece[z, :16, :width]
            w_ref[pl.ds(pl.multiple_of(at + 16, 16), 16)] = piece[z, :16, width:]
        held = feature_slots(column, features // (NZ * NX), slots, 1)
        place = lax.broadcasted_iota(jnp.int32, (features, slots), 0) == held
        total = total + dot(place.astype(jnp.bfloat16), piece[:, 16:].reshape(slots, -1))
    pairs_ref[...] = total.astype(jnp.bfloat16)
    count = pieces[0].shape[0]
    own = pl.multiple_of(place_ref[0] * width, width)
    for i, piece in enumerate(pieces):
        at = pl.ds(pl.multiple_of(place_ref[i] * count, count), count)
        normed = rms_scale(piece[...], gain_ref[...]).astype(jnp.bfloat16)
        query_ref[at, :] = dot(normed, w_ref[...]).astype(jnp.bfloat16)
        residual_ref[at, :] = piece[:, pl.ds(own, width)]


def attention_kernel(place_ref, live_ref, query_ref, w_ref, *refs):
    pieces, out_ref, pair_ref = refs[:-2], refs[-2], refs[-1]
    width = query_ref.shape[1]
    total_rows = query_ref.shape[0]
    for i, piece in enumerate(pieces):
        pair_ref[i] = dot(piece[...], w_ref[...]).astype(jnp.bfloat16)
    out_ref[:SPAN] = jnp.zeros((SPAN, width), jnp.bfloat16)

    def one(i, carry):
        place = place_ref[i]
        first = pl.multiple_of(place * 2 * SPAN + SPAN, SPAN)
        second = pl.multiple_of(jnp.minimum(first + SPAN, total_rows - SPAN), SPAN)
        query = jnp.concatenate([query_ref[pl.ds(first, SPAN)], query_ref[pl.ds(second, SPAN)]])
        upper = lax.broadcasted_iota(jnp.int32, (2 * SPAN, PACK), 0) < SPAN
        in_first = lax.broadcasted_iota(jnp.int32, (2 * SPAN, PACK), 1) < live_ref[place]
        allowed = (upper & in_first) | jnp.logical_not(upper | in_first)
        heads = []
        for h in range(width // HD):
            cols = slice(h * HD, (h + 1) * HD)
            keys = pair_ref[i, :, cols]
            values = pair_ref[i, :, width + h * HD : width + (h + 1) * HD]
            scores = lax.dot_general(query[:, cols], keys, NT, preferred_element_type=jnp.float32)
            scores = jnp.where(allowed, scores * HD ** (-0.5), -jnp.inf)
            largest = jnp.max(scores, axis=-1, keepdims=True)
            powers = jnp.exp(scores - largest)
            totals = jnp.sum(powers, axis=-1, keepdims=True)
            weights = (powers / totals).astype(jnp.bfloat16)
            heads.append(dot(weights, values).astype(jnp.bfloat16))
        result = jnp.concatenate(heads, axis=1)
        out_ref[pl.ds(first, SPAN)] = result[:SPAN]

        @pl.when(place < NY * NC - 1)
        def _():
            out_ref[pl.ds(second, SPAN)] = result[SPAN:]

        return carry

    lax.fori_loop(0, len(pieces), one, 0)


def output_kernel(place_ref, column_ref, residual_ref, *refs):
    head_pieces, pieces = refs[:NX], refs[NX : NX + NY * NC]
    out_ref, w_ref = refs[NX + NY * NC :]
    width = pieces[0].shape[1]
    chunk = 256
    for j, piece in enumerate(head_pieces):
        for z in range(NZ):
            at = pl.multiple_of((z * NX + column_ref[j]) * 32, 32)
            w_ref[pl.ds(at, 32)] = piece[z]

    def one(step, carry):
        at = pl.ds(pl.multiple_of(step * chunk, chunk), chunk)
        total = residual_ref[at].astype(jnp.float32)
        for i, piece in enumerate(pieces):
            depth = pl.ds(pl.multiple_of(place_ref[i] * width, width), width)
            total = total + dot(piece[at], w_ref[depth])
        out_ref[at] = total.astype(jnp.bfloat16)
        return carry

    lax.fori_loop(0, out_ref.shape[0] // chunk, one, 0)


def pad_rows(a, rows):
    return jnp.pad(a, ((0, rows - a.shape[0]), (0, 0)))


def body(
    reader,
    reader_gain,
    database,
    encoder_gain,
    w_expand,
    w_reduce,
    w_query,
    w_key,
    w_value,
    w_output,
    neighbour_ids,
    lengths,
    owners,
):
    bf16 = jnp.bfloat16
    shards = NZ * NX
    seq_index = lax.axis_index("y") * NC + lax.axis_index("c")
    entries, stripe, features = database.shape
    per_row = neighbour_ids.shape[2]

    ids = lax.dynamic_index_in_dim(neighbour_ids, seq_index, 1, keepdims=False)
    token_row = (ids[:, :, None] * stripe + jnp.arange(stripe, dtype=jnp.int32)).reshape(-1)
    stored = database.reshape(entries * stripe, features)
    pick = (token_row[:, None] == jnp.arange(entries * stripe, dtype=jnp.int32)[None]).astype(bf16)
    outgoing = dot(pick, stored).astype(bf16).reshape(shards, per_row * stripe, features)
    arrived = exchange(outgoing, DB)
    arrived = arrived.reshape(shards * per_row * stripe, features)

    padded = 16
    ff_part = pad_rows(jnp.concatenate([w_expand, w_reduce.T], axis=1), padded)
    columns = natural_columns()
    ff_x = gather_x(spread(ff_part, "z", NZ))
    hidden_each = w_expand.shape[1]
    ff_t = call(
        arrange_kernel,
        jax.ShapeDtypeStruct((2 * hidden_each, features), bf16),
        [columns] + ff_x,
        1,
        4 * shards * padded * features * hidden_each,
    )
    ff_pieces = gather_seq(ff_t)

    _, width = w_query.shape
    key_value = pad_rows(jnp.concatenate([w_key, w_value], axis=1), padded)
    halves = jnp.concatenate([w_query[:padded], w_query[padded:]], axis=1)
    head_part = jnp.concatenate([halves, key_value], axis=0)
    head_x = gather_x(spread(head_part, "z", NZ))
    out_x = gather_x(spread(w_output, "z", NZ))

    row_pieces = gather_seq(reader[0])
    places = natural_places()
    seq_len = reader.shape[1] * NY * NC
    model = reader.shape[2]
    half_shape = jax.ShapeDtypeStruct((seq_len, width), bf16)
    queries, residual, w_pairs = call(
        query_kernel,
        (half_shape, half_shape, jax.ShapeDtypeStruct((features, 2 * width), bf16)),
        [places, columns, reader_gain.reshape(1, -1)] + head_x + row_pieces,
        2,
        2 * seq_len * model * width,
        [pltpu.VMEM((model, width), bf16)],
    )

    own_len = lax.dynamic_index_in_dim(lengths[0], seq_index, 0, keepdims=False)
    own_owner = lax.dynamic_index_in_dim(owners[0], seq_index, 0, keepdims=False)
    position = jnp.arange(PACK, dtype=jnp.int32)
    start = jnp.int32(0)
    source_row = jnp.zeros((PACK,), jnp.int32)
    for j in range(per_row):
        token = position - start
        inside = (token >= 0) & (token < own_len[j])
        shard = (own_owner[j] + token // stripe) % shards
        source = (shard * per_row + j) * stripe + token % stripe
        source_row = jnp.where(inside, source, source_row)
        start = start + own_len[j]
    slots = jnp.arange(arrived.shape[0], dtype=jnp.int32)
    packing = (source_row[:, None] == slots[None]).astype(bf16)
    live_rows = dot(packing, arrived).astype(bf16)

    encoded = call(
        feed_forward_kernel,
        jax.ShapeDtypeStruct((PACK, features), bf16),
        [live_rows, encoder_gain.reshape(1, -1)] + ff_pieces,
        0,
        4 * PACK * features * hidden_each * NY * NC,
    )
    encoded_pieces = gather_seq(encoded)
    first_live = lengths[0, :, 0] + lengths[0, :, 1]
    attended = call(
        attention_kernel,
        half_shape,
        [places, first_live, queries, w_pairs] + encoded_pieces,
        2,
        2 * PACK * NY * NC * features * 2 * width,
        [pltpu.VMEM((NY * NC, PACK, 2 * width), bf16)],
    )
    attended_pieces = gather_seq(attended)
    result = call(
        output_kernel,
        half_shape,
        [places, columns, residual] + out_x + attended_pieces,
        2,
        2 * seq_len * model * width,
        [pltpu.VMEM((model, width), bf16)],
    )
    return result[None]


def solution(mesh):
    fine = Mesh(mesh.devices.reshape(NZ, NX, NY, NC), ("z", "x", "y", "c"))
    in_specs = (
        P(DB, SEQ, None),
        P(),
        P(DB, None, None),
        P(),
        P(DB, SEQ),
        P(SEQ, DB),
        P(DB, SEQ),
        P(DB, SEQ),
        P(DB, SEQ),
        P(DB, SEQ),
        P(),
        P(DB, None, None),
        P(DB, None, None),
    )
    out_specs = P(DB, None, SEQ)
    return jax.shard_map(body, mesh=fine, in_specs=in_specs, out_specs=out_specs, check_vma=False)
```

```python
import functools

import jax
import jax.numpy as jnp
from jax import lax
from jax.experimental import pallas as pl
from jax.experimental.pallas import tpu as pltpu
from jax.sharding import Mesh, PartitionSpec as P

HD = 128
SPAN = 64
NZ = 16
NX = 4
NY = 4
NC = 2
PACK = 320
DB = ("z", "x")
SEQ = ("y", "c")


epsilon = 1e-06


def rms_scale(values, scales):
    widened = values.astype(jnp.float32)
    mean_square = jnp.mean(widened * widened, axis=-1, keepdims=True)
    return widened * lax.rsqrt(mean_square + epsilon) * scales


def dot(a, b):
    return jnp.dot(a, b, preferred_element_type=jnp.float32)


def exchange(blocks, axis):
    return lax.all_to_all(blocks, axis, split_axis=0, concat_axis=0, tiled=True)


def spread(part, axis, size):
    return exchange(jnp.broadcast_to(part[None], (size,) + part.shape), axis)


def ring(step):
    return [(i, (i + step) % NY) for i in range(NY)]


def gather_seq(part):
    swap = [(0, 1), (1, 0)]
    near = lax.ppermute(part, "y", ring(-1))
    last = lax.ppermute(part, "y", ring(1))
    far = lax.ppermute(part, "y", ring(2))
    mine = [part, near, far, last]
    return mine + [lax.ppermute(piece, "c", swap) for piece in mine]


def gather_x(part):
    hops = (-1, 2, 1)
    return [part] + [
        lax.ppermute(part, "x", [(i, (i + step) % NX) for i in range(NX)])
        for step in hops
    ]


def natural_columns():
    return ((lax.axis_index("x") + jnp.arange(NX, dtype=jnp.int32)) % NX).astype(jnp.int32)


def natural_places():
    y = lax.axis_index("y")
    c = lax.axis_index("c")
    ahead = (y + jnp.arange(NY, dtype=jnp.int32)) % NY * NC
    return jnp.concatenate([ahead + c, ahead + 1 - c]).astype(jnp.int32)


def fixed_places():
    c = lax.axis_index("c")
    even = jnp.arange(NY, dtype=jnp.int32) * NC
    return jnp.concatenate([even + c, even + 1 - c]).astype(jnp.int32)


def gather_mine(part):
    mine = spread(part, "y", NY)
    return mine, lax.ppermute(mine, "c", [(0, 1), (1, 0)])


def call(kernel, out_shape, operands, scalars, flops, scratch=()):
    size = sum(o.size * o.dtype.itemsize for o in operands)
    return pl.pallas_call(
        kernel,
        out_shape=out_shape,
        in_specs=[pl.BlockSpec(memory_space=pltpu.SMEM)] * scalars
        + [pl.BlockSpec(memory_space=pltpu.VMEM)] * (len(operands) - scalars),
        scratch_shapes=list(scratch),
        cost_estimate=pl.CostEstimate(flops=flops, bytes_accessed=size, transcendentals=0),
    )(*operands)


NT = (((1,), (1,)), ((), ()))


def feed_forward_kernel(packing_ref, arrived_ref, gain_ref, *refs):
    pieces, (out_ref, rows_ref) = refs[:-2], refs[-2:]
    each = pieces[0].shape[0] // 2
    rows_ref[...] = dot(packing_ref[...], arrived_ref[...]).astype(jnp.bfloat16)
    rows = rows_ref[...]
    normed = rms_scale(rows, gain_ref[...]).astype(jnp.bfloat16)
    total = rows.astype(jnp.float32)
    for piece in pieces:
        hidden = lax.dot_general(normed, piece[:each], NT, preferred_element_type=jnp.float32)
        hidden = 0.5 * hidden * (1.0 + lax.erf(hidden * 0.5**0.5))
        total = total + dot(hidden.astype(jnp.bfloat16), piece[each:])
    out_ref[...] = total.astype(jnp.bfloat16)


def feature_slots(column, rows_each, slots, axis):
    shape = (1, slots) if axis == 1 else (slots, 1)
    slot = lax.broadcasted_iota(jnp.int32, shape, axis)
    shard = (slot >> 4) * NX + column
    return jnp.where((slot & 15) < rows_each, shard * rows_each + (slot & 15), -1)


def arrange_kernel(column_ref, *refs):
    pieces, out_ref = refs[:-1], refs[-1]
    features = out_ref.shape[1]
    slots = NZ * 16
    lanes = pieces[0].shape[2]
    total = jnp.zeros((lanes, features), jnp.float32)
    for j, piece in enumerate(pieces):
        held = feature_slots(column_ref[j], features // (NZ * NX), slots, 0)
        place = lax.broadcasted_iota(jnp.int32, (slots, features), 1) == held
        total = total + lax.dot_general(
            piece[...].reshape(slots, -1),
            place.astype(jnp.bfloat16),
            (((0,), (0,)), ((), ())),
            preferred_element_type=jnp.float32,
        )
    total = total.astype(jnp.bfloat16)
    each = out_ref.shape[0] // 2
    out_ref[:each] = total[:each]
    out_ref[each:] = total[lanes // 2 : lanes // 2 + each]


def query_kernel(place_ref, column_ref, gain_ref, *refs):
    head_pieces, pieces = refs[:NX], refs[NX : NX + NY * NC]
    query_ref, residual_ref, pairs_ref, w_ref = refs[NX + NY * NC :]
    width = w_ref.shape[1]
    features = pairs_ref.shape[0]
    slots = NZ * 16
    total = jnp.zeros(pairs_ref.shape, jnp.float32)
    for j, piece in enumerate(head_pieces):
        column = column_ref[j]
        for z in range(NZ):
            at = pl.multiple_of((z * NX + column) * 32, 32)
            w_ref[pl.ds(at, 16)] = piece[z, :16, :width]
            w_ref[pl.ds(pl.multiple_of(at + 16, 16), 16)] = piece[z, :16, width:]
        held = feature_slots(column, features // (NZ * NX), slots, 1)
        place = lax.broadcasted_iota(jnp.int32, (features, slots), 0) == held
        total = total + dot(place.astype(jnp.bfloat16), piece[:, 16:32].reshape(slots, -1))
    pairs_ref[...] = total.astype(jnp.bfloat16)
    count = pieces[0].shape[0]
    own = pl.multiple_of(place_ref[0] * width, width)
    for i, piece in enumerate(pieces):
        at = pl.ds(pl.multiple_of(place_ref[i] * count, count), count)
        normed = rms_scale(piece[...], gain_ref[...]).astype(jnp.bfloat16)
        query_ref[at, :] = dot(normed, w_ref[...]).astype(jnp.bfloat16)
        residual_ref[at, :] = piece[:, pl.ds(own, width)]


def attention_kernel(first_piece, place_ref, live_ref, query_ref, w_ref, *refs):
    before, (piece_ref, out_ref, pair_ref) = refs[:-3], refs[-3:]
    width = query_ref.shape[1]
    total_rows = query_ref.shape[0]
    count = piece_ref.shape[0]
    for i in range(count):
        pair_ref[i] = dot(piece_ref[i], w_ref[...]).astype(jnp.bfloat16)
    if before:
        out_ref[...] = before[0][...]
    else:
        out_ref[:SPAN] = jnp.zeros((SPAN, width), jnp.bfloat16)

    def one(i, carry):
        place = place_ref[first_piece + i]
        first = pl.multiple_of(place * 2 * SPAN + SPAN, SPAN)
        second = pl.multiple_of(jnp.minimum(first + SPAN, total_rows - SPAN), SPAN)
        query = jnp.concatenate([query_ref[pl.ds(first, SPAN)], query_ref[pl.ds(second, SPAN)]])
        upper = lax.broadcasted_iota(jnp.int32, (2 * SPAN, PACK), 0) < SPAN
        in_first = lax.broadcasted_iota(jnp.int32, (2 * SPAN, PACK), 1) < live_ref[place]
        allowed = (upper & in_first) | jnp.logical_not(upper | in_first)
        heads = []
        for h in range(width // HD):
            cols = slice(h * HD, (h + 1) * HD)
            keys = pair_ref[i, :, cols]
            values = pair_ref[i, :, width + h * HD : width + (h + 1) * HD]
            scores = lax.dot_general(query[:, cols], keys, NT, preferred_element_type=jnp.float32)
            scores = jnp.where(allowed, scores * HD ** (-0.5), -jnp.inf)
            largest = jnp.max(scores, axis=-1, keepdims=True)
            powers = jnp.exp(scores - largest)
            totals = jnp.sum(powers, axis=-1, keepdims=True)
            weights = (powers / totals).astype(jnp.bfloat16)
            heads.append(dot(weights, values).astype(jnp.bfloat16))
        result = jnp.concatenate(heads, axis=1)
        out_ref[pl.ds(first, SPAN)] = result[:SPAN]

        @pl.when(place < NY * NC - 1)
        def _():
            out_ref[pl.ds(second, SPAN)] = result[SPAN:]

        return carry

    lax.fori_loop(0, count, one, 0, unroll=2)


def output_kernel(place_ref, column_ref, residual_ref, *refs):
    head_pieces, sides, (out_ref, w_ref) = refs[:NX], refs[NX:-2], refs[-2:]
    width = w_ref.shape[1]
    chunk = 256
    for j, piece in enumerate(head_pieces):
        for z in range(NZ):
            at = pl.multiple_of((z * NX + column_ref[j]) * 32, 32)
            w_ref[pl.ds(at, 16)] = piece[z, 32:, :width]
            w_ref[pl.ds(pl.multiple_of(at + 16, 16), 16)] = piece[z, 32:, width:]

    def one(step, carry):
        at = pl.ds(pl.multiple_of(step * chunk, chunk), chunk)
        total = residual_ref[at].astype(jnp.float32)
        for i in range(NY * NC):
            depth = pl.ds(pl.multiple_of(place_ref[i] * width, width), width)
            total = total + dot(sides[i // NY][i % NY, at], w_ref[depth])
        out_ref[at] = total.astype(jnp.bfloat16)
        return carry

    lax.fori_loop(0, out_ref.shape[0] // chunk, one, 0)


def pad_rows(a, rows):
    return jnp.pad(a, ((0, rows - a.shape[0]), (0, 0)))


def body(
    reader,
    reader_gain,
    database,
    encoder_gain,
    w_expand,
    w_reduce,
    w_query,
    w_key,
    w_value,
    w_output,
    neighbour_ids,
    lengths,
    owners,
):
    bf16 = jnp.bfloat16
    shards = NZ * NX
    seq_index = lax.axis_index("y") * NC + lax.axis_index("c")
    entries, stripe, features = database.shape
    per_row = neighbour_ids.shape[2]

    ids = lax.dynamic_index_in_dim(neighbour_ids, seq_index, 1, keepdims=False)
    token_row = (ids[:, :, None] * stripe + jnp.arange(stripe, dtype=jnp.int32)).reshape(-1)
    stored = database.reshape(entries * stripe, features)
    pick = (token_row[:, None] == jnp.arange(entries * stripe, dtype=jnp.int32)[None]).astype(bf16)
    outgoing = dot(pick, stored).astype(bf16).reshape(shards, per_row * stripe, features)
    arrived = exchange(outgoing, DB)
    arrived = arrived.reshape(shards * per_row * stripe, features)

    rows_each = w_expand.shape[0]
    padded = 16
    _, width = w_query.shape
    hidden_each = w_expand.shape[1]
    gap = ((0, padded - rows_each), (0, width - hidden_each))
    ff_part = jnp.concatenate([jnp.pad(w_expand, gap), jnp.pad(w_reduce.T, gap)], axis=1)
    pair_part = pad_rows(jnp.concatenate([w_key, w_value], axis=1), padded)
    query_part = jnp.concatenate([w_query[:padded], w_query[padded:]], axis=1)
    out_part = jnp.concatenate([w_output[:padded], w_output[padded:]], axis=1)
    part = jnp.concatenate([ff_part, query_part, pair_part, out_part], axis=0)
    weights = spread(part, "z", NZ)
    columns = natural_columns()
    ff_x = gather_x(weights[:, :padded])
    head_x = gather_x(weights[:, padded:])
    ff_t = call(
        arrange_kernel,
        jax.ShapeDtypeStruct((2 * hidden_each, features), bf16),
        [columns] + ff_x,
        1,
        4 * shards * padded * features * hidden_each,
    )
    ff_pieces = gather_seq(ff_t)

    row_pieces = gather_seq(reader[0])
    places = natural_places()
    seq_len = reader.shape[1] * NY * NC
    model = reader.shape[2]
    half_shape = jax.ShapeDtypeStruct((seq_len, width), bf16)
    queries, residual, w_pairs = call(
        query_kernel,
        (half_shape, half_shape, jax.ShapeDtypeStruct((features, 2 * width), bf16)),
        [places, columns, reader_gain.reshape(1, -1)] + head_x + row_pieces,
        2,
        2 * seq_len * model * width,
        [pltpu.VMEM((model, width), bf16)],
    )

    own_len = lax.dynamic_index_in_dim(lengths[0], seq_index, 0, keepdims=False)
    own_owner = lax.dynamic_index_in_dim(owners[0], seq_index, 0, keepdims=False)
    start = jnp.int32(0)
    position = jnp.arange(PACK, dtype=jnp.int32)
    source_row = jnp.zeros((PACK,), jnp.int32)
    for j in range(per_row):
        token = position - start
        inside = (token >= 0) & (token < own_len[j])
        shard = (own_owner[j] + token // stripe) % shards
        source = (shard * per_row + j) * stripe + token % stripe
        source_row = jnp.where(inside, source, source_row)
        start = start + own_len[j]
    slots = jnp.arange(arrived.shape[0], dtype=jnp.int32)
    packing = (source_row[:, None] == slots[None]).astype(bf16)
    encoded = call(
        feed_forward_kernel,
        jax.ShapeDtypeStruct((PACK, features), bf16),
        [packing, arrived, encoder_gain.reshape(1, -1)] + ff_pieces,
        0,
        4 * PACK * features * hidden_each * NY * NC,
        [pltpu.VMEM((PACK, features), bf16)],
    )
    encoded_mine, encoded_other = gather_mine(encoded)
    fixed = fixed_places()
    first_live = lengths[0, :, 0] + lengths[0, :, 1]
    attended = []
    for first_piece, side in ((0, encoded_mine), (NY, encoded_other)):
        attended = [
            call(
                functools.partial(attention_kernel, first_piece),
                half_shape,
                [fixed, first_live, queries, w_pairs] + attended + [side],
                2,
                PACK * NY * NC * features * 2 * width,
                [pltpu.VMEM((NY, PACK, 2 * width), bf16)],
            )
        ]
    attended_sides = gather_mine(attended[0])
    result = call(
        output_kernel,
        half_shape,
        [fixed, columns, residual] + head_x + list(attended_sides),
        2,
        2 * seq_len * model * width,
        [pltpu.VMEM((model, width), bf16)],
    )
    return result[None]


def solution(mesh):
    fine = Mesh(mesh.devices.reshape(NZ, NX, NY, NC), ("z", "x", "y", "c"))
    in_specs = (
        P(DB, SEQ, None),
        P(),
        P(DB, None, None),
        P(),
        P(DB, SEQ),
        P(SEQ, DB),
        P(DB, SEQ),
        P(DB, SEQ),
        P(DB, SEQ),
        P(DB, SEQ),
        P(),
        P(DB, None, None),
        P(DB, None, None),
    )
    out_specs = P(DB, None, SEQ)
    return jax.shard_map(body, mesh=fine, in_specs=in_specs, out_specs=out_specs, check_vma=False)
```

```python
import functools

import jax
import jax.numpy as jnp
from jax import lax
from jax.experimental import pallas as pl
from jax.experimental.pallas import tpu as pltpu
from jax.sharding import Mesh, PartitionSpec as P

HD = 128
SPAN = 64
NZ = 16
NX = 4
NY = 4
NC = 2
PACK = 320
DB = ("z", "x")
SEQ = ("y", "c")


epsilon = 1e-06


def rms_scale(values, scales):
    widened = values.astype(jnp.float32)
    mean_square = jnp.mean(widened * widened, axis=-1, keepdims=True)
    return widened * lax.rsqrt(mean_square + epsilon) * scales


def dot(a, b):
    return jnp.dot(a, b, preferred_element_type=jnp.float32)


def exchange(blocks, axis):
    return lax.all_to_all(blocks, axis, split_axis=0, concat_axis=0, tiled=True)


def spread(part, axis, size):
    return exchange(jnp.broadcast_to(part[None], (size,) + part.shape), axis)


def ring(step):
    return [(i, (i + step) % NY) for i in range(NY)]


def gather_seq(part):
    swap = [(0, 1), (1, 0)]
    near = lax.ppermute(part, "y", ring(-1))
    last = lax.ppermute(part, "y", ring(1))
    far = lax.ppermute(part, "y", ring(2))
    mine = [part, near, far, last]
    return mine + [lax.ppermute(piece, "c", swap) for piece in mine]


def gather_x(part):
    hops = (-1, 2, 1)
    return [part] + [
        lax.ppermute(part, "x", [(i, (i + step) % NX) for i in range(NX)])
        for step in hops
    ]


def natural_columns():
    return ((lax.axis_index("x") + jnp.arange(NX, dtype=jnp.int32)) % NX).astype(jnp.int32)


def natural_places():
    y = lax.axis_index("y")
    c = lax.axis_index("c")
    ahead = (y + jnp.arange(NY, dtype=jnp.int32)) % NY * NC
    return jnp.concatenate([ahead + c, ahead + 1 - c]).astype(jnp.int32)


def fixed_places():
    c = lax.axis_index("c")
    even = jnp.arange(NY, dtype=jnp.int32) * NC
    return jnp.concatenate([even + c, even + 1 - c]).astype(jnp.int32)


def gather_mine(part):
    mine = spread(part, "y", NY)
    return mine, lax.ppermute(mine, "c", [(0, 1), (1, 0)])


def call(kernel, out_shape, operands, scalars, flops, scratch=()):
    size = sum(o.size * o.dtype.itemsize for o in operands)
    return pl.pallas_call(
        kernel,
        out_shape=out_shape,
        in_specs=[pl.BlockSpec(memory_space=pltpu.SMEM)] * scalars
        + [pl.BlockSpec(memory_space=pltpu.VMEM)] * (len(operands) - scalars),
        scratch_shapes=list(scratch),
        cost_estimate=pl.CostEstimate(flops=flops, bytes_accessed=size, transcendentals=0),
    )(*operands)


NT = (((1,), (1,)), ((), ()))


def feed_forward_kernel(packing_ref, arrived_ref, gain_ref, *refs):
    pieces, (out_ref, rows_ref) = refs[:-2], refs[-2:]
    each = pieces[0].shape[0] // 2
    rows_ref[...] = dot(packing_ref[...], arrived_ref[...]).astype(jnp.bfloat16)
    rows = rows_ref[...]
    normed = rms_scale(rows, gain_ref[...]).astype(jnp.bfloat16)
    total = rows.astype(jnp.float32)
    for piece in pieces:
        hidden = lax.dot_general(normed, piece[:each], NT, preferred_element_type=jnp.float32)
        hidden = 0.5 * hidden * (1.0 + lax.erf(hidden * 0.5**0.5))
        total = total + dot(hidden.astype(jnp.bfloat16), piece[each:])
    out_ref[...] = total.astype(jnp.bfloat16)


def feature_slots(column, rows_each, slots, axis):
    shape = (1, slots) if axis == 1 else (slots, 1)
    slot = lax.broadcasted_iota(jnp.int32, shape, axis)
    shard = (slot >> 4) * NX + column
    return jnp.where((slot & 15) < rows_each, shard * rows_each + (slot & 15), -1)


def arrange_kernel(column_ref, *refs):
    pieces, out_ref = refs[:-1], refs[-1]
    features = out_ref.shape[1]
    slots = NZ * 16
    lanes = pieces[0].shape[2]
    total = jnp.zeros((lanes, features), jnp.float32)
    for j, piece in enumerate(pieces):
        held = feature_slots(column_ref[j], features // (NZ * NX), slots, 0)
        place = lax.broadcasted_iota(jnp.int32, (slots, features), 1) == held
        total = total + lax.dot_general(
            piece[...].reshape(slots, -1),
            place.astype(jnp.bfloat16),
            (((0,), (0,)), ((), ())),
            preferred_element_type=jnp.float32,
        )
    total = total.astype(jnp.bfloat16)
    each = out_ref.shape[0] // 2
    out_ref[:each] = total[:each]
    out_ref[each:] = total[lanes // 2 : lanes // 2 + each]


def query_kernel(place_ref, column_ref, gain_ref, *refs):
    head_pieces, pieces = refs[:NX], refs[NX : NX + NY * NC]
    query_ref, residual_ref, pairs_ref, w_ref = refs[NX + NY * NC :]
    width = w_ref.shape[1]
    features = pairs_ref.shape[0]
    slots = NZ * 16
    total = jnp.zeros(pairs_ref.shape, jnp.float32)
    for j, piece in enumerate(head_pieces):
        column = column_ref[j]
        for z in range(NZ):
            at = pl.multiple_of((z * NX + column) * 32, 32)
            w_ref[pl.ds(at, 16)] = piece[z, :16, :width]
            w_ref[pl.ds(pl.multiple_of(at + 16, 16), 16)] = piece[z, :16, width:]
        held = feature_slots(column, features // (NZ * NX), slots, 1)
        place = lax.broadcasted_iota(jnp.int32, (features, slots), 0) == held
        total = total + dot(place.astype(jnp.bfloat16), piece[:, 16:].reshape(slots, -1))
    pairs_ref[...] = total.astype(jnp.bfloat16)
    count = pieces[0].shape[0]
    own = pl.multiple_of(place_ref[0] * width, width)
    for i, piece in enumerate(pieces):
        at = pl.ds(pl.multiple_of(place_ref[i] * count, count), count)
        normed = rms_scale(piece[...], gain_ref[...]).astype(jnp.bfloat16)
        query_ref[at, :] = dot(normed, w_ref[...]).astype(jnp.bfloat16)
        residual_ref[at, :] = piece[:, pl.ds(own, width)]


def attention_kernel(first_piece, place_ref, live_ref, query_ref, w_ref, *refs):
    before, pieces, (out_ref, pair_ref) = refs[: -NY - 2], refs[-NY - 2 : -2], refs[-2:]
    width = query_ref.shape[1]
    total_rows = query_ref.shape[0]
    count = len(pieces)
    for i, piece in enumerate(pieces):
        pair_ref[i] = dot(piece[...], w_ref[...]).astype(jnp.bfloat16)
    if before:
        out_ref[...] = before[0][...]
    else:
        out_ref[:SPAN] = jnp.zeros((SPAN, width), jnp.bfloat16)

    def one(i, carry):
        place = place_ref[first_piece + i]
        first = pl.multiple_of(place * 2 * SPAN + SPAN, SPAN)
        second = pl.multiple_of(jnp.minimum(first + SPAN, total_rows - SPAN), SPAN)
        query = jnp.concatenate([query_ref[pl.ds(first, SPAN)], query_ref[pl.ds(second, SPAN)]])
        upper = lax.broadcasted_iota(jnp.int32, (2 * SPAN, PACK), 0) < SPAN
        in_first = lax.broadcasted_iota(jnp.int32, (2 * SPAN, PACK), 1) < live_ref[place]
        allowed = (upper & in_first) | jnp.logical_not(upper | in_first)
        heads = []
        for h in range(width // HD):
            cols = slice(h * HD, (h + 1) * HD)
            keys = pair_ref[i, :, cols]
            values = pair_ref[i, :, width + h * HD : width + (h + 1) * HD]
            scores = lax.dot_general(query[:, cols], keys, NT, preferred_element_type=jnp.float32)
            scores = jnp.where(allowed, scores * HD ** (-0.5), -jnp.inf)
            largest = jnp.max(scores, axis=-1, keepdims=True)
            powers = jnp.exp(scores - largest)
            totals = jnp.sum(powers, axis=-1, keepdims=True)
            weights = (powers / totals).astype(jnp.bfloat16)
            heads.append(dot(weights, values).astype(jnp.bfloat16))
        result = jnp.concatenate(heads, axis=1)
        out_ref[pl.ds(first, SPAN)] = result[:SPAN]

        @pl.when(place < NY * NC - 1)
        def _():
            out_ref[pl.ds(second, SPAN)] = result[SPAN:]

        return carry

    lax.fori_loop(0, count, one, 0, unroll=2)


def output_rows(place_ref, first_piece, side, w_ref, base_ref, out_ref):
    width = w_ref.shape[1]
    chunk = 256

    def one(step, carry):
        at = pl.ds(pl.multiple_of(step * chunk, chunk), chunk)
        total = base_ref[at].astype(jnp.float32)
        for i in range(NY):
            depth = pl.multiple_of(place_ref[first_piece + i] * width, width)
            total = total + dot(side[i, at], w_ref[pl.ds(depth, width)])
        out_ref[at] = total.astype(out_ref.dtype)
        return carry

    lax.fori_loop(0, out_ref.shape[0] // chunk, one, 0)


def out_weight_kernel(column_ref, *refs):
    head_pieces, w_ref = refs[:-1], refs[-1]
    width = w_ref.shape[1]
    for j, piece in enumerate(head_pieces):
        for z in range(NZ):
            at = pl.multiple_of((z * NX + column_ref[j]) * 32, 32)
            w_ref[pl.ds(at, 16)] = piece[z, :, :width]
            w_ref[pl.ds(pl.multiple_of(at + 16, 16), 16)] = piece[z, :, width:]


def first_output_kernel(place_ref, residual_ref, w_ref, side, out_ref):
    output_rows(place_ref, 0, side, w_ref, residual_ref, out_ref)


def second_output_kernel(place_ref, partial_ref, w_ref, side, out_ref):
    output_rows(place_ref, NY, side, w_ref, partial_ref, out_ref)


def pad_rows(a, rows):
    return jnp.pad(a, ((0, rows - a.shape[0]), (0, 0)))


def body(
    reader,
    reader_gain,
    database,
    encoder_gain,
    w_expand,
    w_reduce,
    w_query,
    w_key,
    w_value,
    w_output,
    neighbour_ids,
    lengths,
    owners,
):
    bf16 = jnp.bfloat16
    shards = NZ * NX
    seq_index = lax.axis_index("y") * NC + lax.axis_index("c")
    entries, stripe, features = database.shape
    per_row = neighbour_ids.shape[2]

    ids = lax.dynamic_index_in_dim(neighbour_ids, seq_index, 1, keepdims=False)
    token_row = (ids[:, :, None] * stripe + jnp.arange(stripe, dtype=jnp.int32)).reshape(-1)
    stored = database.reshape(entries * stripe, features)
    pick = (token_row[:, None] == jnp.arange(entries * stripe, dtype=jnp.int32)[None]).astype(bf16)
    outgoing = dot(pick, stored).astype(bf16).reshape(shards, per_row * stripe, features)
    arrived = exchange(outgoing, DB)
    arrived = arrived.reshape(shards * per_row * stripe, features)

    rows_each = w_expand.shape[0]
    padded = 16
    _, width = w_query.shape
    hidden_each = w_expand.shape[1]
    gap = ((0, padded - rows_each), (0, width - hidden_each))
    ff_part = jnp.concatenate([jnp.pad(w_expand, gap), jnp.pad(w_reduce.T, gap)], axis=1)
    pair_part = pad_rows(jnp.concatenate([w_key, w_value], axis=1), padded)
    query_part = jnp.concatenate([w_query[:padded], w_query[padded:]], axis=1)
    out_part = jnp.concatenate([w_output[:padded], w_output[padded:]], axis=1)
    columns = natural_columns()
    ff_x = gather_x(spread(ff_part, "z", NZ))
    head_part = jnp.concatenate([query_part, pair_part], axis=0)
    head_x = gather_x(spread(head_part, "z", NZ))
    out_x = gather_x(spread(out_part, "z", NZ))
    ff_t = call(
        arrange_kernel,
        jax.ShapeDtypeStruct((2 * hidden_each, features), bf16),
        [columns] + ff_x,
        1,
        4 * shards * padded * features * hidden_each,
    )
    ff_pieces = gather_seq(ff_t)

    row_pieces = gather_seq(reader[0])
    places = natural_places()
    seq_len = reader.shape[1] * NY * NC
    model = reader.shape[2]
    half_shape = jax.ShapeDtypeStruct((seq_len, width), bf16)
    queries, residual, w_pairs = call(
        query_kernel,
        (half_shape, half_shape, jax.ShapeDtypeStruct((features, 2 * width), bf16)),
        [places, columns, reader_gain.reshape(1, -1)] + head_x + row_pieces,
        2,
        2 * seq_len * model * width,
        [pltpu.VMEM((model, width), bf16)],
    )

    own_len = lax.dynamic_index_in_dim(lengths[0], seq_index, 0, keepdims=False)
    own_owner = lax.dynamic_index_in_dim(owners[0], seq_index, 0, keepdims=False)
    start = jnp.int32(0)
    position = jnp.arange(PACK, dtype=jnp.int32)
    source_row = jnp.zeros((PACK,), jnp.int32)
    for j in range(per_row):
        token = position - start
        inside = (token >= 0) & (token < own_len[j])
        shard = (own_owner[j] + token // stripe) % shards
        source = (shard * per_row + j) * stripe + token % stripe
        source_row = jnp.where(inside, source, source_row)
        start = start + own_len[j]
    slots = jnp.arange(arrived.shape[0], dtype=jnp.int32)
    packing = (source_row[:, None] == slots[None]).astype(bf16)
    encoded = call(
        feed_forward_kernel,
        jax.ShapeDtypeStruct((PACK, features), bf16),
        [packing, arrived, encoder_gain.reshape(1, -1)] + ff_pieces,
        0,
        4 * PACK * features * hidden_each * NY * NC,
        [pltpu.VMEM((PACK, features), bf16)],
    )
    encoded_pieces = gather_seq(encoded)
    fixed = fixed_places()
    first_live = lengths[0, :, 0] + lengths[0, :, 1]
    attended = []
    for first_piece in (0, NY):
        attended = [
            call(
                functools.partial(attention_kernel, first_piece),
                half_shape,
                [places, first_live, queries, w_pairs]
                + attended
                + encoded_pieces[first_piece : first_piece + NY],
                2,
                PACK * NY * NC * features * 2 * width,
                [pltpu.VMEM((NY, PACK, 2 * width), bf16)],
            )
        ]
    attended_mine, attended_other = gather_mine(attended[0])
    w_o = call(
        out_weight_kernel,
        jax.ShapeDtypeStruct((model, width), bf16),
        [columns] + out_x,
        1,
        model * width,
    )
    partial = call(
        first_output_kernel,
        jax.ShapeDtypeStruct((seq_len, width), jnp.float32),
        [fixed, residual, w_o, attended_mine],
        1,
        seq_len * model * width,
    )
    result = call(
        second_output_kernel,
        half_shape,
        [fixed, partial, w_o, attended_other],
        1,
        seq_len * model * width,
    )
    return result[None]


def solution(mesh):
    fine = Mesh(mesh.devices.reshape(NZ, NX, NY, NC), ("z", "x", "y", "c"))
    in_specs = (
        P(DB, SEQ, None),
        P(),
        P(DB, None, None),
        P(),
        P(DB, SEQ),
        P(SEQ, DB),
        P(DB, SEQ),
        P(DB, SEQ),
        P(DB, SEQ),
        P(DB, SEQ),
        P(),
        P(DB, None, None),
        P(DB, None, None),
    )
    out_specs = P(DB, None, SEQ)
    return jax.shard_map(body, mesh=fine, in_specs=in_specs, out_specs=out_specs, check_vma=False)
```
